32 devices in a mesh: groups: 2 (over x), frame: 16 (over z, y, core).
Axes of the slice: x: 2, y: 2, z: 4, core: 2. Of those that a mesh axis runs over, the one named last changes fastest.
Arguments:
- latent: bfloat16 [128, 32, 1152], P(('groups', 'frame')), parts along dimension 0, may hold values from -6 to 6
- ln_gain: float32 [1152], replicated, may hold values from 0.1 to 1.9
- q_gain: float32 [72], replicated, may hold values from 0.1 to 1.9
- k_gain: float32 [72], replicated, may hold values from 0.1 to 1.9
- w_qkv: bfloat16 [1152, 3456], replicated, may hold values from -0.1875 to 0.1875
- w_out: bfloat16 [1152, 1152], replicated, may hold values from -0.5 to 0.5
Outputs:
- result: bfloat16 [128, 32, 1152], P(('groups', 'frame')), parts along dimension 0
The draws below stay inside these ranges and needn't reach their ends.
There are 2 independent parts, one for each index of `groups`. The reference program is written for one: setup_inputs(seed, part) draws one part's arguments, and reference() takes and returns one part's arrays. A program takes and returns all parts, laid end to end along the dimension named above; an argument that names none is the same for every part. Nothing has to cross between parts.
All inputs are finite; a program needn't handle non-finite values.
Results may differ from the reference program's by a relative error of at most 0.006.
Values may be sent and summed in bfloat16 or wider, within the bound.
A program may use at most 64 MiB of HBM per device.

```python
import jax
import jax.numpy as jnp
from jax import lax

D = 1152
HEADS = 16
HEAD_DIM = 72
LAT_W = 32
WIN_ROWS = 4
FRAMES = 16


def block_levels(own_key, extent, shards, smallest, top_value):
    def one(axis_at, parts):
        steps = jax.random.uniform(jax.random.fold_in(jax.random.fold_in(own_key, 6), axis_at), (parts,), jnp.float32, smallest / len(shards), top_value / len(shards))
        return jnp.repeat(jnp.exp(steps), extent[axis_at] // parts).reshape((-1,) + (1,) * (len(extent) - axis_at - 1))

    level = one(*shards[0])
    for cut in shards[1:]:
        level = level * one(*cut)
    return level


def gaussian(own_key, shape, scale, limit, split=(), held_as=jnp.bfloat16):
    values = scale * jax.random.normal(own_key, shape, jnp.float32)
    if split:
        values = values * block_levels(own_key, shape, split, -0.22, 0.18)
    return jnp.clip(values, -limit, limit).astype(held_as)


def setup_inputs(seed: int = 0, part: int = 0) -> dict:
    arg_keys = jax.random.split(jax.random.key(seed), 7)
    part_splits = jax.random.split(jax.random.fold_in(arg_keys[6], part), 7)
    return {
        "latent": gaussian(part_splits[0], (FRAMES * WIN_ROWS, LAT_W, D), 1.0, 6.0, ((0, 16),)),
        "ln_gain": jnp.clip(1.0 + 0.18 * jax.random.normal(arg_keys[1], (D,), jnp.float32), 0.1, 1.9),
        "q_gain": jnp.clip(1.0 + 0.18 * jax.random.normal(arg_keys[2], (HEAD_DIM,), jnp.float32), 0.1, 1.9),
        "k_gain": jnp.clip(1.0 + 0.18 * jax.random.normal(arg_keys[3], (HEAD_DIM,), jnp.float32), 0.1, 1.9),
        "w_qkv": gaussian(arg_keys[4], (D, 3 * D), D ** -0.5, 0.1875),
        "w_out": gaussian(arg_keys[5], (D, D), (D // 8) ** -0.5, 0.5),
    }


def layer_norm(rows, ln_gain):
    values = rows.astype(jnp.float32)
    center = values - lax.optimization_barrier(jnp.mean(values, axis=-1, keepdims=True))
    spread = lax.optimization_barrier(jnp.mean(center * center, axis=-1, keepdims=True))
    return (center * lax.rsqrt(spread + 1e-06) * ln_gain).astype(jnp.bfloat16)

def head_norm(values, gain):
    shaped = values.reshape(values.shape[:-1] + (HEADS, HEAD_DIM))
    mean_sq = lax.optimization_barrier(jnp.mean(shaped * shaped, axis=-1, keepdims=True))
    return (shaped * lax.rsqrt(mean_sq + 1e-06) * gain).astype(jnp.bfloat16).reshape(values.shape)

def project(normed, w_qkv, q_gain, k_gain):
    width = normed.shape[-1]
    mixed = jnp.dot(normed.reshape(-1, width), w_qkv, preferred_element_type=jnp.float32)
    mixed = mixed.reshape(normed.shape[:-1] + (3 * width,))
    query = head_norm(mixed[..., :width], q_gain)
    keys = head_norm(mixed[..., width:2 * width], k_gain)
    values = mixed[..., 2 * width:].astype(jnp.bfloat16)
    return (query, keys, values)

def attend(query, keys, values):
    lead = query.shape[0]
    others = query.shape[1]
    q_four = query.reshape(lead, others, HEADS, HEAD_DIM).astype(jnp.float32)
    k_four = keys.reshape(lead, others, HEADS, HEAD_DIM).astype(jnp.float32)
    v_four = values.reshape(lead, others, HEADS, HEAD_DIM).astype(jnp.float32)
    scores = jnp.einsum('tshe,ushe->shtu', q_four, k_four) * HEAD_DIM ** (-0.5)
    weights = jnp.exp(scores)
    weights = (weights / lax.optimization_barrier(jnp.sum(weights, axis=-1, keepdims=True))).astype(jnp.bfloat16)
    mixed = jnp.einsum('shtu,ushe->tshe', weights.astype(jnp.float32), v_four)
    return mixed.astype(jnp.bfloat16).reshape(query.shape)

def reference(latent, ln_gain, q_gain, k_gain, w_qkv, w_out):
    frame_count = latent.shape[0] // WIN_ROWS
    grid = latent.reshape(frame_count, WIN_ROWS, LAT_W, D)

    def one_row(slab):
        normed = layer_norm(slab, ln_gain)
        query, keys, values = project(normed, w_qkv, q_gain, k_gain)
        mixed = attend(query, keys, values)
        branch = jnp.dot(mixed.reshape(-1, D), w_out, preferred_element_type=jnp.float32)
        return (slab.astype(jnp.float32) + branch.reshape(slab.shape)).astype(jnp.bfloat16)
    result = lax.map(one_row, jnp.swapaxes(grid, 0, 1))
    return jnp.swapaxes(result, 0, 1).reshape(latent.shape)
```

```python
import functools

import jax
import jax.numpy as jnp
from jax import lax
from jax.experimental import pallas as pl
from jax.experimental.pallas import tpu as pltpu
from jax.sharding import PartitionSpec as P

HEADS = 16
HEAD_DIM = 72
LANES = 128
IN_CUTS = (0, 512, 1024, 1152)
OUT_CUTS = (0, 256, 768, 1152)
MESH = pl.DeviceIdType.MESH
F32 = jnp.float32
BF16 = jnp.bfloat16


def split_dot(values, ones):
    high = values.astype(BF16)
    low = (values - high.astype(F32)).astype(BF16)
    return jnp.dot(high, ones, preferred_element_type=F32) + jnp.dot(
        low, ones, preferred_element_type=F32
    )


def kernel(
    n,
    lat_ref,
    ln_ref,
    qg_ref,
    kg_ref,
    wq_hbm,
    wo_hbm,
    out_ref,
    xs,
    xr,
    ys,
    yr,
    wq,
    wo,
    acc,
    qn,
    kn,
    vb,
    wq_sem,
    wo_sem,
    s1,
    r1,
    s2,
    r2,
):
    rows, columns, model = lat_ref.shape
    tokens = rows * columns
    per = tokens // n
    me = lax.axis_index("frame")
    in_parts = list(zip(IN_CUTS[:-1], IN_CUTS[1:]))
    out_parts = list(zip(OUT_CUTS[:-1], OUT_CUTS[1:]))

    barrier = pltpu.get_barrier_semaphore()

    def greet(k, _):
        pl.semaphore_signal(
            barrier, inc=1, device_id={"frame": lax.rem(me + k, n)}, device_id_type=MESH
        )
        return 0

    lax.fori_loop(1, n, greet, 0)

    loads = []
    for c, (a, b) in enumerate(in_parts):
        loads.append(
            pltpu.make_async_copy(wq_hbm.at[pl.ds(a, b - a)], wq.at[pl.ds(a, b - a)], wq_sem.at[c])
        )
        loads[-1].start()
    load_out = pltpu.make_async_copy(wo_hbm, wo, wo_sem)
    load_out.start()

    values = lat_ref[...].astype(F32).reshape(tokens, model)
    center = values - jnp.mean(values, axis=-1, keepdims=True)
    spread = jnp.mean(center * center, axis=-1, keepdims=True)
    normed = center * lax.rsqrt(spread + 1e-06) * ln_ref[...]
    xs[...] = normed.reshape(n, per, model).astype(BF16)
    xr[pl.ds(me, 1)] = xs[pl.ds(me, 1)]

    pl.semaphore_wait(barrier, n - 1)

    def copy(src, dst, send, recv, c, a, b, k, to, slot):
        return pltpu.make_async_remote_copy(
            src_ref=src.at[to, :, pl.ds(a, b - a)],
            dst_ref=dst.at[slot, :, pl.ds(a, b - a)],
            send_sem=send.at[c, k],
            recv_sem=recv.at[c, k],
            device_id={"frame": to},
            device_id_type=MESH,
        )

    def send_all(src, dst, send, recv, c, a, b):
        def one(k, _):
            copy(src, dst, send, recv, c, a, b, k, lax.rem(me + k, n), me).start()
            return 0

        lax.fori_loop(1, n, one, 0)

    def wait_recv_all(src, dst, send, recv, c, a, b):
        def one(k, _):
            copy(
                src, dst, send, recv, c, a, b, k, lax.rem(me + k, n), lax.rem(me + n - k, n)
            ).wait_recv()
            return 0

        lax.fori_loop(1, n, one, 0)

    def wait_send_all(src, dst, send, recv, c, a, b):
        def one(k, _):
            copy(src, dst, send, recv, c, a, b, k, lax.rem(me + k, n), me).wait_send()
            return 0

        lax.fori_loop(1, n, one, 0)

    for c, (a, b) in enumerate(in_parts):
        send_all(xs, xr, s1, r1, c, a, b)

    lane = lax.broadcasted_iota(jnp.int32, (model, LANES), 0)
    head = lax.broadcasted_iota(jnp.int32, (model, LANES), 1)
    gather = ((lane >= head * HEAD_DIM) & (lane < (head + 1) * HEAD_DIM)).astype(F32).astype(BF16)
    head_t = lax.broadcasted_iota(jnp.int32, (LANES, model), 0)
    lane_t = lax.broadcasted_iota(jnp.int32, (LANES, model), 1)
    inside = (lane_t >= head_t * HEAD_DIM) & (lane_t < (head_t + 1) * HEAD_DIM)
    spread_t = inside.astype(F32).astype(BF16)
    entry = lax.broadcasted_iota(jnp.int32, (HEAD_DIM, model), 0)
    place = lax.broadcasted_iota(jnp.int32, (HEAD_DIM, model), 1)
    picked = entry == place
    for h in range(1, HEADS):
        picked = picked | (entry + h * HEAD_DIM == place)
    repeat = picked.astype(F32)

    def whole_gain(ref):
        rows8 = jnp.broadcast_to(ref[...], (8, HEAD_DIM))
        return jnp.dot(
            rows8, repeat, preferred_element_type=F32, precision=lax.Precision.HIGHEST
        )[0:1]

    q_gain = whole_gain(qg_ref)
    k_gain = whole_gain(kg_ref)

    width = 3 * model
    step = model // 3
    for c, (a, b) in enumerate(in_parts):
        wait_recv_all(xs, xr, s1, r1, c, a, b)
        loads[c].wait()
        part = xr[:, :, a:b].astype(F32).reshape(tokens, b - a).astype(BF16)
        for col in range(0, width, step):
            product = jnp.dot(part, wq[a:b, col : col + step], preferred_element_type=F32)
            if c == 0:
                acc[:, col : col + step] = product
            else:
                acc[:, col : col + step] += product

    def head_norm(block, gain):
        sums = split_dot(block * block, gather)
        scale = lax.rsqrt(sums * (1.0 / HEAD_DIM) + 1e-06)
        return (block * split_dot(scale, spread_t) * gain).astype(BF16)

    qn[...] = head_norm(acc[:, :model], q_gain)
    kn[...] = head_norm(acc[:, model : 2 * model], k_gain)
    vb[...] = acc[:, 2 * model :].astype(BF16)

    row_i = lax.broadcasted_iota(jnp.int32, (tokens, tokens), 0)
    col_i = lax.broadcasted_iota(jnp.int32, (tokens, tokens), 1)
    same = lax.rem(row_i, per) == lax.rem(col_i, per)

    def head_mask(h, lo, hi):
        at = lax.broadcasted_iota(jnp.int32, (tokens, hi - lo), 1) + lo
        return (at >= h * HEAD_DIM) & (at < (h + 1) * HEAD_DIM)

    probs = {}

    def attend(h):
        lo = h * HEAD_DIM // LANES * LANES
        hi = -(-(h + 1) * HEAD_DIM // LANES) * LANES
        mask = head_mask(h, lo, hi)
        query = jnp.where(mask, qn[:, lo:hi].astype(F32), 0.0).astype(BF16)
        scores = lax.dot_general(
            query, kn[:, lo:hi], (((1,), (1,)), ((), ())), preferred_element_type=F32
        ) * (HEAD_DIM**-0.5)
        weights = jnp.where(same, jnp.exp(scores), 0.0)
        total = jnp.sum(weights, axis=-1, keepdims=True)
        probs[h] = (weights * (1.0 / total)).astype(BF16)

    for c, (a, b) in enumerate(out_parts):
        for tile in range(a, b, LANES):
            out_tile = None
            for h in range(tile // HEAD_DIM, (tile + LANES - 1) // HEAD_DIM + 1):
                if h not in probs:
                    attend(h)
                mask = head_mask(h, tile, tile + LANES)
                value = jnp.where(mask, vb[:, tile : tile + LANES].astype(F32), 0.0).astype(BF16)
                term = jnp.dot(probs[h], value, preferred_element_type=F32)
                out_tile = term if out_tile is None else out_tile + term
            ys[:, :, tile : tile + LANES] = out_tile.reshape(n, per, LANES).astype(BF16)
        send_all(ys, yr, s2, r2, c, a, b)
    yr[pl.ds(me, 1)] = ys[pl.ds(me, 1)]

    load_out.wait()
    branch = lat_ref[...].astype(F32).reshape(tokens, model)
    for c, (a, b) in enumerate(out_parts):
        wait_recv_all(ys, yr, s2, r2, c, a, b)
        part = yr[:, :, a:b].astype(F32).reshape(tokens, b - a).astype(BF16)
        product = jnp.dot(part, wo[a:b, :], preferred_element_type=F32)
        if c == 0:
            acc[:, :model] = product
        elif c < len(out_parts) - 1:
            acc[:, :model] += product
        else:
            product = acc[:, :model] + product
            out_ref[...] = (branch + product).reshape(rows, columns, model).astype(BF16)

    for c, (a, b) in enumerate(in_parts):
        wait_send_all(xs, xr, s1, r1, c, a, b)
    for c, (a, b) in enumerate(out_parts):
        wait_send_all(ys, yr, s2, r2, c, a, b)


def fused(n, latent, ln_gain, q_gain, k_gain, w_qkv, w_out):
    rows, columns, model = latent.shape
    tokens = rows * columns
    per = tokens // n
    vmem = pl.BlockSpec(memory_space=pltpu.VMEM)
    hbm = pl.BlockSpec(memory_space=pl.ANY)
    block = pltpu.VMEM((n, per, model), BF16)
    ins, outs = len(IN_CUTS) - 1, len(OUT_CUTS) - 1
    return pl.pallas_call(
        functools.partial(kernel, n),
        out_shape=jax.ShapeDtypeStruct(latent.shape, BF16),
        in_specs=[vmem, vmem, vmem, vmem, hbm, hbm],
        out_specs=vmem,
        scratch_shapes=[
            block,
            block,
            block,
            block,
            pltpu.VMEM(w_qkv.shape, BF16),
            pltpu.VMEM(w_out.shape, BF16),
            pltpu.VMEM((tokens, w_qkv.shape[1]), F32),
            pltpu.VMEM((tokens, model), BF16),
            pltpu.VMEM((tokens, model), BF16),
            pltpu.VMEM((tokens, model), BF16),
            pltpu.SemaphoreType.DMA((ins,)),
            pltpu.SemaphoreType.DMA,
            pltpu.SemaphoreType.DMA((ins, n)),
            pltpu.SemaphoreType.DMA((ins, n)),
            pltpu.SemaphoreType.DMA((outs, n)),
            pltpu.SemaphoreType.DMA((outs, n)),
        ],
        compiler_params=pltpu.CompilerParams(
            collective_id=0, has_side_effects=True, vmem_limit_bytes=60 * 2**20
        ),
    )(
        latent,
        ln_gain.reshape(1, -1),
        q_gain.reshape(1, -1),
        k_gain.reshape(1, -1),
        w_qkv,
        w_out,
    )


def layer_norm(rows, ln_gain):
    values = rows.astype(jnp.float32)
    center = values - jnp.mean(values, axis=-1, keepdims=True)
    spread = jnp.mean(center * center, axis=-1, keepdims=True)
    return (center * lax.rsqrt(spread + 1e-06) * ln_gain).astype(jnp.bfloat16)


def head_norm(values, gain):
    shaped = values.reshape(values.shape[:-1] + (HEADS, HEAD_DIM))
    mean_sq = jnp.mean(shaped * shaped, axis=-1, keepdims=True)
    return (shaped * lax.rsqrt(mean_sq + 1e-06) * gain).astype(jnp.bfloat16).reshape(values.shape)


def project(normed, w_qkv, q_gain, k_gain):
    width = normed.shape[-1]
    mixed = jnp.dot(normed.reshape(-1, width), w_qkv, preferred_element_type=jnp.float32)
    mixed = mixed.reshape(normed.shape[:-1] + (3 * width,))
    query = head_norm(mixed[..., :width], q_gain)
    keys = head_norm(mixed[..., width : 2 * width], k_gain)
    values = mixed[..., 2 * width :].astype(jnp.bfloat16)
    return (query, keys, values)


def attend(query, keys, values):
    lead = query.shape[0]
    others = query.shape[1]
    q_four = query.reshape(lead, others, HEADS, HEAD_DIM)
    k_four = keys.reshape(lead, others, HEADS, HEAD_DIM)
    v_four = values.reshape(lead, others, HEADS, HEAD_DIM)
    scores = jnp.einsum(
        "tshe,ushe->shtu", q_four, k_four, preferred_element_type=jnp.float32
    ) * HEAD_DIM ** (-0.5)
    weights = jnp.exp(scores)
    weights = (weights / jnp.sum(weights, axis=-1, keepdims=True)).astype(jnp.bfloat16)
    mixed = jnp.einsum("shtu,ushe->tshe", weights, v_four, preferred_element_type=jnp.float32)
    return mixed.astype(jnp.bfloat16).reshape(query.shape)


def body(latent, ln_gain, q_gain, k_gain, w_qkv, w_out):
    device_count = lax.axis_size("frame")
    rows, columns, model = latent.shape
    positions = rows * columns
    per_peer = positions // device_count
    if per_peer % 8 == 0:
        return fused(device_count, latent, ln_gain, q_gain, k_gain, w_qkv, w_out)
    flat = latent.reshape(positions, model)
    normed = layer_norm(flat, ln_gain)
    query, keys, values = project(
        lax.all_to_all(
            normed.reshape(device_count, per_peer, model),
            "frame",
            split_axis=0,
            concat_axis=0,
            tiled=True,
        ),
        w_qkv,
        q_gain,
        k_gain,
    )
    mixed = attend(query, keys, values)
    returned = lax.all_to_all(mixed, "frame", split_axis=0, concat_axis=0, tiled=True)
    attended = returned.reshape(positions, model)
    branch = jnp.dot(attended, w_out, preferred_element_type=jnp.float32)
    result = flat.astype(jnp.float32) + branch
    return result.astype(jnp.bfloat16).reshape(latent.shape)


def solution(mesh):
    placed = (P(("groups", "frame"), None, None), P(), P(), P(), P(), P())
    return jax.shard_map(
        body,
        mesh=mesh,
        in_specs=placed,
        out_specs=P(("groups", "frame"), None, None),
        check_vma=False,
    )
```

```python
import functools

import jax
import jax.numpy as jnp
from jax import lax
from jax.experimental import pallas as pl
from jax.experimental.pallas import tpu as pltpu
from jax.sharding import PartitionSpec as P

HEADS = 16
HEAD_DIM = 72
LANES = 128
IN_CUTS = (0, 512, 1024, 1152)
MID_CUTS = (0, 384, 768, 1152)
OUT_CUTS = (0, 256, 640, 1152)
SPAN = 512
VMEM_BYTES = 66600000
MESH = pl.DeviceIdType.MESH
F32 = jnp.float32
BF16 = jnp.bfloat16


def kernel(
    n,
    lat_hbm,
    ln_ref,
    qg_ref,
    kg_ref,
    wq_hbm,
    wo_hbm,
    out_ref,
    lat,
    xs,
    xr,
    ys,
    yr,
    wq,
    wo,
    acc,
    qn,
    kn,
    lat_sem,
    wq_sem,
    wo_sem,
    s1,
    r1,
    s2,
    r2,
):
    rows, columns, model = lat_hbm.shape
    tokens = rows * columns
    per = tokens // n
    me = lax.axis_index("frame")
    in_parts = list(zip(IN_CUTS[:-1], IN_CUTS[1:]))
    out_parts = list(zip(OUT_CUTS[:-1], OUT_CUTS[1:]))

    barrier = pltpu.get_barrier_semaphore()

    def offset(i):
        return n // 2 + (1 - 2 * lax.rem(i, 2)) * ((i + 1) // 2)

    def greet(i, _):
        pl.semaphore_signal(
            barrier,
            inc=1,
            device_id={"frame": lax.rem(me + offset(i), n)},
            device_id_type=MESH,
        )
        return 0

    lax.fori_loop(0, n - 1, greet, 0)

    load_lat = pltpu.make_async_copy(lat_hbm, lat, lat_sem)
    load_lat.start()
    loads = []
    for c, (a, b) in enumerate(in_parts):
        loads.append(
            pltpu.make_async_copy(wq_hbm.at[pl.ds(a, b - a)], wq.at[pl.ds(a, b - a)], wq_sem.at[c])
        )
        loads[-1].start()
    load_out = pltpu.make_async_copy(wo_hbm, wo, wo_sem)
    load_out.start()

    load_lat.wait()
    values = lat[...].astype(F32).reshape(tokens, model)
    center = values - jnp.mean(values, axis=-1, keepdims=True)
    spread = jnp.mean(center * center, axis=-1, keepdims=True)
    normed = center * lax.rsqrt(spread + 1e-06) * ln_ref[...].reshape(1, model)
    xs[...] = normed.reshape(n, per, model).astype(BF16)
    xr[pl.ds(me, 1)] = xs[pl.ds(me, 1)]

    pl.semaphore_wait(barrier, n - 1)

    def copy(src, dst, send, recv, c, a, b, k, to, slot):
        return pltpu.make_async_remote_copy(
            src_ref=src.at[to, :, pl.ds(a, b - a)],
            dst_ref=dst.at[slot, :, pl.ds(a, b - a)],
            send_sem=send.at[c, k],
            recv_sem=recv.at[c, k],
            device_id={"frame": to},
            device_id_type=MESH,
        )

    def send_all(src, dst, send, recv, c, a, b):
        def one(i, _):
            k = offset(i)
            copy(src, dst, send, recv, c, a, b, k, lax.rem(me + k, n), me).start()
            return 0

        lax.fori_loop(0, n - 1, one, 0)

    def wait_recv_all(src, dst, send, recv, c, a, b):
        def one(k, _):
            copy(
                src, dst, send, recv, c, a, b, k, lax.rem(me + k, n), lax.rem(me + n - k, n)
            ).wait_recv()
            return 0

        lax.fori_loop(1, n, one, 0)

    def wait_send_all(src, dst, send, recv, c, a, b):
        def one(k, _):
            copy(src, dst, send, recv, c, a, b, k, lax.rem(me + k, n), me).wait_send()
            return 0

        lax.fori_loop(1, n, one, 0)

    for c, (a, b) in enumerate(in_parts):
        send_all(xs, xr, s1, r1, c, a, b)

    entry = lax.broadcasted_iota(jnp.int32, (HEAD_DIM, model), 0)
    place = lax.broadcasted_iota(jnp.int32, (HEAD_DIM, model), 1)
    picked = entry == place
    for h in range(1, HEADS):
        picked = picked | (entry + h * HEAD_DIM == place)
    repeat = picked.astype(F32)

    def whole_gain(ref):
        rows8 = jnp.broadcast_to(ref[...].reshape(1, HEAD_DIM), (8, HEAD_DIM))
        return jnp.dot(
            rows8, repeat, preferred_element_type=F32, precision=lax.Precision.HIGHEST
        )[0:1]

    q_gain = whole_gain(qg_ref)
    k_gain = whole_gain(kg_ref)

    row_i = lax.broadcasted_iota(jnp.int32, (tokens, tokens), 0)
    col_i = lax.broadcasted_iota(jnp.int32, (tokens, tokens), 1)
    same = lax.rem(row_i, per) == lax.rem(col_i, per)

    def arrived(c, a, b):
        wait_recv_all(xs, xr, s1, r1, c, a, b)
        loads[c].wait()
        return xr[:, :, a:b].astype(F32).reshape(tokens, b - a).astype(BF16)

    width = 3 * model
    step = model // 3
    for c, (a, b) in enumerate(in_parts[:-1]):
        part = arrived(c, a, b)
        for col in range(0, width, step):
            product = jnp.dot(part, wq[a:b, col : col + step], preferred_element_type=F32)
            if c == 0:
                acc[:, col : col + step] = product
            else:
                acc[:, col : col + step] += product

    last, (a_in, b_in) = len(in_parts) - 1, in_parts[-1]
    part = arrived(last, a_in, b_in)

    def head_mask(h, lo, hi):
        at = lax.broadcasted_iota(jnp.int32, (tokens, hi - lo), 1) + lo
        return (at >= h * HEAD_DIM) & (at < (h + 1) * HEAD_DIM)

    probs = {}
    done = 0
    for c, (a, b) in enumerate(out_parts):
        piece = slice(MID_CUTS[c], MID_CUTS[c + 1])
        for third in range(3):
            cols = slice(third * model + piece.start, third * model + piece.stop)
            acc[:, cols] += jnp.dot(part, wq[a_in:b_in, cols], preferred_element_type=F32)

        first, done = done, piece.stop // HEAD_DIM
        count = done - first
        lo = first * HEAD_DIM // LANES * LANES
        hi = -(-done * HEAD_DIM // LANES) * LANES
        span = hi - lo
        lane = lax.broadcasted_iota(jnp.int32, (span, LANES), 0) + lo
        head = lax.broadcasted_iota(jnp.int32, (span, LANES), 1)
        start = (head + first) * HEAD_DIM
        gather = ((head < count) & (lane >= start) & (lane < start + HEAD_DIM)).astype(F32)
        gather = gather.astype(BF16)
        head = lax.rem(lax.broadcasted_iota(jnp.int32, (2 * LANES, span), 0), LANES)
        lane = lax.broadcasted_iota(jnp.int32, (2 * LANES, span), 1) + lo
        start = (head + first) * HEAD_DIM
        expand = ((head < count) & (lane >= start) & (lane < start + HEAD_DIM)).astype(F32)
        expand = expand.astype(BF16)

        def head_norm(base, gain):
            block = acc[:, base + lo : base + hi]
            sums = jnp.dot((block * block).astype(BF16), gather, preferred_element_type=F32)
            scale = lax.rsqrt(sums * (1.0 / HEAD_DIM) + 1e-06)
            high = scale.astype(BF16)
            low = (scale - high.astype(F32)).astype(BF16)
            scale = jnp.dot(
                jnp.concatenate([high, low], axis=1), expand, preferred_element_type=F32
            )
            return (block * scale * gain[:, lo:hi]).astype(BF16)

        qn[:, :span] = head_norm(0, q_gain)
        kn[:, :span] = head_norm(model, k_gain)

        for h in range(first, done):
            at = h * HEAD_DIM // LANES * LANES
            end = -(-(h + 1) * HEAD_DIM // LANES) * LANES
            mask = head_mask(h, at, end)
            query = jnp.where(mask, qn[:, at - lo : end - lo].astype(F32), 0.0).astype(BF16)
            scores = lax.dot_general(
                query,
                kn[:, at - lo : end - lo],
                (((1,), (1,)), ((), ())),
                preferred_element_type=F32,
            ) * (HEAD_DIM**-0.5)
            weights = jnp.where(same, jnp.exp(scores), 0.0)
            total = jnp.sum(weights, axis=-1, keepdims=True)
            probs[h] = (weights * (1.0 / total)).astype(BF16)

        for tile in range(a, b, LANES):
            out_tile = None
            for h in range(tile // HEAD_DIM, (tile + LANES - 1) // HEAD_DIM + 1):
                mask = head_mask(h, tile, tile + LANES)
                value = acc[:, 2 * model + tile : 2 * model + tile + LANES]
                value = jnp.where(mask, value, 0.0).astype(BF16)
                term = jnp.dot(probs[h], value, preferred_element_type=F32)
                out_tile = term if out_tile is None else out_tile + term
            ys[:, :, tile : tile + LANES] = out_tile.reshape(n, per, LANES).astype(BF16)
        send_all(ys, yr, s2, r2, c, a, b)
    yr[pl.ds(me, 1)] = ys[pl.ds(me, 1)]

    load_out.wait()
    for c, (a, b) in enumerate(in_parts):
        wait_send_all(xs, xr, s1, r1, c, a, b)
    for c, (a, b) in enumerate(out_parts):
        wait_recv_all(ys, yr, s2, r2, c, a, b)
        part = yr[:, :, a:b].astype(F32).reshape(tokens, b - a).astype(BF16)
        product = jnp.dot(part, wo[a:b, :], preferred_element_type=F32)
        if c == 0:
            acc[:, :model] = product
        elif c < len(out_parts) - 1:
            acc[:, :model] += product
        else:
            branch = lat[...].astype(F32).reshape(tokens, model)
            product = acc[:, :model] + product
            out_ref[...] = (branch + product).reshape(rows, columns, model).astype(BF16)
    for c, (a, b) in enumerate(out_parts):
        wait_send_all(ys, yr, s2, r2, c, a, b)


def fused(n, latent, ln_gain, q_gain, k_gain, w_qkv, w_out):
    rows, columns, model = latent.shape
    tokens = rows * columns
    per = tokens // n
    vmem = pl.BlockSpec(memory_space=pltpu.VMEM)
    hbm = pl.BlockSpec(memory_space=pltpu.HBM)
    block = pltpu.VMEM((n, per, model), BF16)
    ins, outs = len(IN_CUTS) - 1, len(OUT_CUTS) - 1
    return pl.pallas_call(
        functools.partial(kernel, n),
        out_shape=jax.ShapeDtypeStruct(latent.shape, BF16),
        in_specs=[hbm, vmem, vmem, vmem, hbm, hbm],
        out_specs=vmem,
        scratch_shapes=[
            pltpu.VMEM(latent.shape, BF16),
            block,
            block,
            block,
            block,
            pltpu.VMEM(w_qkv.shape, BF16),
            pltpu.VMEM(w_out.shape, BF16),
            pltpu.VMEM((tokens, w_qkv.shape[1]), F32),
            pltpu.VMEM((tokens, SPAN), BF16),
            pltpu.VMEM((tokens, SPAN), BF16),
            pltpu.SemaphoreType.DMA,
            pltpu.SemaphoreType.DMA((ins,)),
            pltpu.SemaphoreType.DMA,
            pltpu.SemaphoreType.DMA((ins, n)),
            pltpu.SemaphoreType.DMA((ins, n)),
            pltpu.SemaphoreType.DMA((outs, n)),
            pltpu.SemaphoreType.DMA((outs, n)),
        ],
        compiler_params=pltpu.CompilerParams(
            collective_id=0, has_side_effects=True, vmem_limit_bytes=VMEM_BYTES
        ),
    )(latent, ln_gain, q_gain, k_gain, w_qkv, w_out)


def layer_norm(rows, ln_gain):
    values = rows.astype(jnp.float32)
    center = values - jnp.mean(values, axis=-1, keepdims=True)
    spread = jnp.mean(center * center, axis=-1, keepdims=True)
    return (center * lax.rsqrt(spread + 1e-06) * ln_gain).astype(jnp.bfloat16)


def head_norm(values, gain):
    shaped = values.reshape(values.shape[:-1] + (HEADS, HEAD_DIM))
    mean_sq = jnp.mean(shaped * shaped, axis=-1, keepdims=True)
    return (shaped * lax.rsqrt(mean_sq + 1e-06) * gain).astype(jnp.bfloat16).reshape(values.shape)


def project(normed, w_qkv, q_gain, k_gain):
    width = normed.shape[-1]
    mixed = jnp.dot(normed.reshape(-1, width), w_qkv, preferred_element_type=jnp.float32)
    mixed = mixed.reshape(normed.shape[:-1] + (3 * width,))
    query = head_norm(mixed[..., :width], q_gain)
    keys = head_norm(mixed[..., width : 2 * width], k_gain)
    values = mixed[..., 2 * width :].astype(jnp.bfloat16)
    return (query, keys, values)


def attend(query, keys, values):
    lead = query.shape[0]
    others = query.shape[1]
    q_four = query.reshape(lead, others, HEADS, HEAD_DIM)
    k_four = keys.reshape(lead, others, HEADS, HEAD_DIM)
    v_four = values.reshape(lead, others, HEADS, HEAD_DIM)
    scores = jnp.einsum(
        "tshe,ushe->shtu", q_four, k_four, preferred_element_type=jnp.float32
    ) * HEAD_DIM ** (-0.5)
    weights = jnp.exp(scores)
    weights = (weights / jnp.sum(weights, axis=-1, keepdims=True)).astype(jnp.bfloat16)
    mixed = jnp.einsum("shtu,ushe->tshe", weights, v_four, preferred_element_type=jnp.float32)
    return mixed.astype(jnp.bfloat16).reshape(query.shape)


def body(latent, ln_gain, q_gain, k_gain, w_qkv, w_out):
    device_count = lax.axis_size("frame")
    rows, columns, model = latent.shape
    positions = rows * columns
    per_peer = positions // device_count
    if per_peer % 8 == 0:
        return fused(device_count, latent, ln_gain, q_gain, k_gain, w_qkv, w_out)
    flat = latent.reshape(positions, model)
    normed = layer_norm(flat, ln_gain)
    query, keys, values = project(
        lax.all_to_all(
            normed.reshape(device_count, per_peer, model),
            "frame",
            split_axis=0,
            concat_axis=0,
            tiled=True,
        ),
        w_qkv,
        q_gain,
        k_gain,
    )
    mixed = attend(query, keys, values)
    returned = lax.all_to_all(mixed, "frame", split_axis=0, concat_axis=0, tiled=True)
    attended = returned.reshape(positions, model)
    branch = jnp.dot(attended, w_out, preferred_element_type=jnp.float32)
    result = flat.astype(jnp.float32) + branch
    return result.astype(jnp.bfloat16).reshape(latent.shape)


def solution(mesh):
    placed = (P(("groups", "frame"), None, None), P(), P(), P(), P(), P())
    return jax.shard_map(
        body,
        mesh=mesh,
        in_specs=placed,
        out_specs=P(("groups", "frame"), None, None),
        check_vma=False,
    )
```

```python
import functools

import jax
import jax.numpy as jnp
from jax import lax
from jax.experimental import pallas as pl
from jax.experimental.pallas import tpu as pltpu
from jax.sharding import PartitionSpec as P

HEADS = 16
HEAD_DIM = 72
LANES = 128
IN_CUTS = (0, 512, 1024, 1152)
MID_CUTS = (0, 384, 768, 1152)
OUT_CUTS = (0, 256, 640, 1152)
SPAN = 512
VMEM_BYTES = 30000000
MESH = pl.DeviceIdType.MESH
F32 = jnp.float32
BF16 = jnp.bfloat16


def kernel(
    n,
    lat_hbm,
    ln_hbm,
    qg_hbm,
    kg_hbm,
    wq_hbm,
    wo_hbm,
    out_ref,
    lat,
    ln_ref,
    qg_ref,
    kg_ref,
    xs,
    xr,
    ys,
    yr,
    wq,
    wo,
    acc,
    qn,
    kn,
    lat_sem,
    gain_sem,
    wq_sem,
    wo_sem,
    s1,
    r1,
    s2,
    r2,
):
    rows, columns, model = lat_hbm.shape
    tokens = rows * columns
    per = tokens // n
    me = lax.axis_index("frame")
    in_parts = list(zip(IN_CUTS[:-1], IN_CUTS[1:]))
    out_parts = list(zip(OUT_CUTS[:-1], OUT_CUTS[1:]))

    barrier = pltpu.get_barrier_semaphore()

    def offset(i):
        return n // 2 + (1 - 2 * lax.rem(i, 2)) * ((i + 1) // 2)

    def greet(i, _):
        pl.semaphore_signal(
            barrier,
            inc=1,
            device_id={"frame": lax.rem(me + offset(i), n)},
            device_id_type=MESH,
        )
        return 0

    lax.fori_loop(0, n - 1, greet, 0)

    load_lat = pltpu.make_async_copy(lat_hbm, lat, lat_sem)
    load_lat.start()
    gains = [
        pltpu.make_async_copy(src, dst, gain_sem.at[i])
        for i, (src, dst) in enumerate(((ln_hbm, ln_ref), (qg_hbm, qg_ref), (kg_hbm, kg_ref)))
    ]
    for load in gains:
        load.start()
    loads = []
    for c, (a, b) in enumerate(in_parts):
        loads.append(
            pltpu.make_async_copy(wq_hbm.at[pl.ds(a, b - a)], wq.at[pl.ds(a, b - a)], wq_sem.at[c])
        )
        loads[-1].start()
    load_out = pltpu.make_async_copy(wo_hbm, wo, wo_sem)
    load_out.start()

    load_lat.wait()
    for load in gains:
        load.wait()
    values = lat[...].astype(F32).reshape(tokens, model)
    center = values - jnp.mean(values, axis=-1, keepdims=True)
    spread = jnp.mean(center * center, axis=-1, keepdims=True)
    normed = center * lax.rsqrt(spread + 1e-06) * ln_ref[...].reshape(1, model)
    xs[...] = normed.reshape(n, per, model).astype(BF16)
    xr[pl.ds(me, 1)] = xs[pl.ds(me, 1)]

    pl.semaphore_wait(barrier, n - 1)

    def copy(src, dst, send, recv, c, a, b, k, to, slot):
        return pltpu.make_async_remote_copy(
            src_ref=src.at[to, :, pl.ds(a, b - a)],
            dst_ref=dst.at[slot, :, pl.ds(a, b - a)],
            send_sem=send.at[c, k],
            recv_sem=recv.at[c, k],
            device_id={"frame": to},
            device_id_type=MESH,
        )

    def send_all(src, dst, send, recv, c, a, b):
        def one(i, _):
            k = offset(i)
            copy(src, dst, send, recv, c, a, b, k, lax.rem(me + k, n), me).start()
            return 0

        lax.fori_loop(0, n - 1, one, 0)

    def wait_recv_all(src, dst, send, recv, c, a, b):
        def one(k, _):
            copy(
                src, dst, send, recv, c, a, b, k, lax.rem(me + k, n), lax.rem(me + n - k, n)
            ).wait_recv()
            return 0

        lax.fori_loop(1, n, one, 0)

    def wait_send_all(src, dst, send, recv, c, a, b):
        def one(k, _):
            copy(src, dst, send, recv, c, a, b, k, lax.rem(me + k, n), me).wait_send()
            return 0

        lax.fori_loop(1, n, one, 0)

    for c, (a, b) in enumerate(in_parts):
        send_all(xs, xr, s1, r1, c, a, b)

    entry = lax.broadcasted_iota(jnp.int32, (HEAD_DIM, model), 0)
    place = lax.broadcasted_iota(jnp.int32, (HEAD_DIM, model), 1)
    picked = entry == place
    for h in range(1, HEADS):
        picked = picked | (entry + h * HEAD_DIM == place)
    repeat = picked.astype(F32)

    def whole_gain(ref):
        rows8 = jnp.broadcast_to(ref[...].reshape(1, HEAD_DIM), (8, HEAD_DIM))
        return jnp.dot(
            rows8, repeat, preferred_element_type=F32, precision=lax.Precision.HIGHEST
        )[0:1]

    q_gain = whole_gain(qg_ref)
    k_gain = whole_gain(kg_ref)

    row_i = lax.broadcasted_iota(jnp.int32, (tokens, tokens), 0)
    col_i = lax.broadcasted_iota(jnp.int32, (tokens, tokens), 1)
    same = lax.rem(row_i, per) == lax.rem(col_i, per)

    def arrived(c, a, b):
        wait_recv_all(xs, xr, s1, r1, c, a, b)
        loads[c].wait()
        return xr[:, :, a:b].astype(F32).reshape(tokens, b - a).astype(BF16)

    width = 3 * model
    step = model // 3
    for c, (a, b) in enumerate(in_parts[:-1]):
        part = arrived(c, a, b)
        for col in range(0, width, step):
            product = jnp.dot(part, wq[a:b, col : col + step], preferred_element_type=F32)
            if c == 0:
                acc[:, col : col + step] = product
            else:
                acc[:, col : col + step] += product

    last, (a_in, b_in) = len(in_parts) - 1, in_parts[-1]
    part = arrived(last, a_in, b_in)

    def head_mask(h, lo, hi):
        at = lax.broadcasted_iota(jnp.int32, (tokens, hi - lo), 1) + lo
        return (at >= h * HEAD_DIM) & (at < (h + 1) * HEAD_DIM)

    probs = {}
    done = 0
    for c, (a, b) in enumerate(out_parts):
        piece = slice(MID_CUTS[c], MID_CUTS[c + 1])
        for third in range(3):
            cols = slice(third * model + piece.start, third * model + piece.stop)
            acc[:, cols] += jnp.dot(part, wq[a_in:b_in, cols], preferred_element_type=F32)

        first, done = done, piece.stop // HEAD_DIM
        count = done - first
        lo = first * HEAD_DIM // LANES * LANES
        hi = -(-done * HEAD_DIM // LANES) * LANES
        span = hi - lo
        lane = lax.broadcasted_iota(jnp.int32, (span, LANES), 0) + lo
        head = lax.broadcasted_iota(jnp.int32, (span, LANES), 1)
        start = (head + first) * HEAD_DIM
        gather = ((head < count) & (lane >= start) & (lane < start + HEAD_DIM)).astype(F32)
        gather = gather.astype(BF16)
        head = lax.rem(lax.broadcasted_iota(jnp.int32, (2 * LANES, span), 0), LANES)
        lane = lax.broadcasted_iota(jnp.int32, (2 * LANES, span), 1) + lo
        start = (head + first) * HEAD_DIM
        expand = ((head < count) & (lane >= start) & (lane < start + HEAD_DIM)).astype(F32)
        expand = expand.astype(BF16)

        def head_norm(base, gain):
            block = acc[:, base + lo : base + hi]
            square = block * block
            high = square.astype(BF16)
            low = (square - high.astype(F32)).astype(BF16)
            sums = jnp.dot(high, gather, preferred_element_type=F32)
            sums += jnp.dot(low, gather, preferred_element_type=F32)
            scale = lax.rsqrt(sums * (1.0 / HEAD_DIM) + 1e-06)
            high = scale.astype(BF16)
            low = (scale - high.astype(F32)).astype(BF16)
            scale = jnp.dot(
                jnp.concatenate([high, low], axis=1), expand, preferred_element_type=F32
            )
            return (block * scale * gain[:, lo:hi]).astype(BF16)

        qn[:, :span] = head_norm(0, q_gain)
        kn[:, :span] = head_norm(model, k_gain)

        for h in range(first, done):
            at = h * HEAD_DIM // LANES * LANES
            end = -(-(h + 1) * HEAD_DIM // LANES) * LANES
            mask = head_mask(h, at, end)
            query = jnp.where(mask, qn[:, at - lo : end - lo].astype(F32), 0.0).astype(BF16)
            scores = lax.dot_general(
                query,
                kn[:, at - lo : end - lo],
                (((1,), (1,)), ((), ())),
                preferred_element_type=F32,
            ) * (HEAD_DIM**-0.5)
            weights = jnp.where(same, jnp.exp(scores), 0.0)
            total = jnp.sum(weights, axis=-1, keepdims=True)
            probs[h] = (weights * (1.0 / total)).astype(BF16)

        for tile in range(a, b, LANES):
            out_tile = None
            for h in range(tile // HEAD_DIM, (tile + LANES - 1) // HEAD_DIM + 1):
                mask = head_mask(h, tile, tile + LANES)
                value = acc[:, 2 * model + tile : 2 * model + tile + LANES]
                value = jnp.where(mask, value, 0.0).astype(BF16)
                term = jnp.dot(probs[h], value, preferred_element_type=F32)
                out_tile = term if out_tile is None else out_tile + term
            ys[:, :, tile : tile + LANES] = out_tile.reshape(n, per, LANES).astype(BF16)
        send_all(ys, yr, s2, r2, c, a, b)
    yr[pl.ds(me, 1)] = ys[pl.ds(me, 1)]

    load_out.wait()
    for c, (a, b) in enumerate(in_parts):
        wait_send_all(xs, xr, s1, r1, c, a, b)
    for c, (a, b) in enumerate(out_parts):
        wait_recv_all(ys, yr, s2, r2, c, a, b)
        part = yr[:, :, a:b].astype(F32).reshape(tokens, b - a).astype(BF16)
        product = jnp.dot(part, wo[a:b, :], preferred_element_type=F32)
        if c == 0:
            acc[:, :model] = product
        elif c < len(out_parts) - 1:
            acc[:, :model] += product
        else:
            branch = lat[...].astype(F32).reshape(tokens, model)
            product = acc[:, :model] + product
            out_ref[...] = (branch + product).reshape(rows, columns, model).astype(BF16)
    for c, (a, b) in enumerate(out_parts):
        wait_send_all(ys, yr, s2, r2, c, a, b)


def fused(n, latent, ln_gain, q_gain, k_gain, w_qkv, w_out):
    rows, columns, model = latent.shape
    tokens = rows * columns
    per = tokens // n
    vmem = pl.BlockSpec(memory_space=pltpu.VMEM)
    hbm = pl.BlockSpec(memory_space=pltpu.HBM)
    block = pltpu.VMEM((n, per, model), BF16)
    ins, outs = len(IN_CUTS) - 1, len(OUT_CUTS) - 1
    return pl.pallas_call(
        functools.partial(kernel, n),
        out_shape=jax.ShapeDtypeStruct(latent.shape, BF16),
        in_specs=[hbm] * 6,
        out_specs=vmem,
        scratch_shapes=[
            pltpu.VMEM(latent.shape, BF16),
            pltpu.VMEM(ln_gain.shape, F32),
            pltpu.VMEM(q_gain.shape, F32),
            pltpu.VMEM(k_gain.shape, F32),
            block,
            block,
            block,
            block,
            pltpu.VMEM(w_qkv.shape, BF16),
            pltpu.VMEM(w_out.shape, BF16),
            pltpu.VMEM((tokens, w_qkv.shape[1]), F32),
            pltpu.VMEM((tokens, SPAN), BF16),
            pltpu.VMEM((tokens, SPAN), BF16),
            pltpu.SemaphoreType.DMA,
            pltpu.SemaphoreType.DMA((3,)),
            pltpu.SemaphoreType.DMA((ins,)),
            pltpu.SemaphoreType.DMA,
            pltpu.SemaphoreType.DMA((ins, n)),
            pltpu.SemaphoreType.DMA((ins, n)),
            pltpu.SemaphoreType.DMA((outs, n)),
            pltpu.SemaphoreType.DMA((outs, n)),
        ],
        compiler_params=pltpu.CompilerParams(
            collective_id=0, has_side_effects=True, vmem_limit_bytes=VMEM_BYTES
        ),
    )(
        *(
            pltpu.with_memory_space_constraint(value, pltpu.HBM)
            for value in (latent, ln_gain, q_gain, k_gain, w_qkv, w_out)
        )
    )


def layer_norm(rows, ln_gain):
    values = rows.astype(jnp.float32)
    center = values - jnp.mean(values, axis=-1, keepdims=True)
    spread = jnp.mean(center * center, axis=-1, keepdims=True)
    return (center * lax.rsqrt(spread + 1e-06) * ln_gain).astype(jnp.bfloat16)


def head_norm(values, gain):
    shaped = values.reshape(values.shape[:-1] + (HEADS, HEAD_DIM))
    mean_sq = jnp.mean(shaped * shaped, axis=-1, keepdims=True)
    return (shaped * lax.rsqrt(mean_sq + 1e-06) * gain).astype(jnp.bfloat16).reshape(values.shape)


def project(normed, w_qkv, q_gain, k_gain):
    width = normed.shape[-1]
    mixed = jnp.dot(normed.reshape(-1, width), w_qkv, preferred_element_type=jnp.float32)
    mixed = mixed.reshape(normed.shape[:-1] + (3 * width,))
    query = head_norm(mixed[..., :width], q_gain)
    keys = head_norm(mixed[..., width : 2 * width], k_gain)
    values = mixed[..., 2 * width :].astype(jnp.bfloat16)
    return (query, keys, values)


def attend(query, keys, values):
    lead = query.shape[0]
    others = query.shape[1]
    q_four = query.reshape(lead, others, HEADS, HEAD_DIM)
    k_four = keys.reshape(lead, others, HEADS, HEAD_DIM)
    v_four = values.reshape(lead, others, HEADS, HEAD_DIM)
    scores = jnp.einsum(
        "tshe,ushe->shtu", q_four, k_four, preferred_element_type=jnp.float32
    ) * HEAD_DIM ** (-0.5)
    weights = jnp.exp(scores)
    weights = (weights / jnp.sum(weights, axis=-1, keepdims=True)).astype(jnp.bfloat16)
    mixed = jnp.einsum("shtu,ushe->tshe", weights, v_four, preferred_element_type=jnp.float32)
    return mixed.astype(jnp.bfloat16).reshape(query.shape)


def body(latent, ln_gain, q_gain, k_gain, w_qkv, w_out):
    device_count = lax.axis_size("frame")
    rows, columns, model = latent.shape
    positions = rows * columns
    per_peer = positions // device_count
    if per_peer % 8 == 0:
        return fused(device_count, latent, ln_gain, q_gain, k_gain, w_qkv, w_out)
    flat = latent.reshape(positions, model)
    normed = layer_norm(flat, ln_gain)
    query, keys, values = project(
        lax.all_to_all(
            normed.reshape(device_count, per_peer, model),
            "frame",
            split_axis=0,
            concat_axis=0,
            tiled=True,
        ),
        w_qkv,
        q_gain,
        k_gain,
    )
    mixed = attend(query, keys, values)
    returned = lax.all_to_all(mixed, "frame", split_axis=0, concat_axis=0, tiled=True)
    attended = returned.reshape(positions, model)
    branch = jnp.dot(attended, w_out, preferred_element_type=jnp.float32)
    result = flat.astype(jnp.float32) + branch
    return result.astype(jnp.bfloat16).reshape(latent.shape)


def solution(mesh):
    placed = (P(("groups", "frame"), None, None), P(), P(), P(), P(), P())
    return jax.shard_map(
        body,
        mesh=mesh,
        in_specs=placed,
        out_specs=P(("groups", "frame"), None, None),
        check_vma=False,
    )
```

```python
import functools

import jax
import jax.numpy as jnp
from jax import lax
from jax.experimental import pallas as pl
from jax.experimental.pallas import tpu as pltpu
from jax.sharding import PartitionSpec as P

HEADS = 16
HEAD_DIM = 72
LANES = 128
IN_CUTS = (0, 640, 1152)
MID_CUTS = (0, 384, 768, 1152)
OUT_CUTS = (0, 256, 640, 1152)
SPAN = 512
VMEM_BYTES = 30000000
MESH = pl.DeviceIdType.MESH
F32 = jnp.float32
BF16 = jnp.bfloat16


def kernel(
    n,
    lat_hbm,
    ln_hbm,
    qg_hbm,
    kg_hbm,
    wq_hbm,
    wo_hbm,
    out_ref,
    lat,
    ln_ref,
    qg_ref,
    kg_ref,
    xs,
    xr,
    ys,
    yr,
    wq,
    wo,
    acc,
    qn,
    kn,
    lat_sem,
    gain_sem,
    wq_sem,
    wo_sem,
    s1,
    r1,
    s2,
    r2,
):
    rows, columns, model = lat_hbm.shape
    tokens = rows * columns
    per = tokens // n
    me = lax.axis_index("frame")
    in_parts = list(zip(IN_CUTS[:-1], IN_CUTS[1:]))
    out_parts = list(zip(OUT_CUTS[:-1], OUT_CUTS[1:]))

    barrier = pltpu.get_barrier_semaphore()

    steps = sorted(range(1, n), key=lambda k: (abs(k - n // 2), k))
    peers = [lax.rem(me + k, n) for k in steps]
    for to in peers:
        pl.semaphore_signal(barrier, inc=1, device_id={"frame": to}, device_id_type=MESH)

    load_lat = pltpu.make_async_copy(lat_hbm, lat, lat_sem)
    load_lat.start()
    gains = [
        pltpu.make_async_copy(src, dst, gain_sem.at[i])
        for i, (src, dst) in enumerate(((ln_hbm, ln_ref), (qg_hbm, qg_ref), (kg_hbm, kg_ref)))
    ]
    for load in gains:
        load.start()
    loads = []
    for c, (a, b) in enumerate(in_parts):
        loads.append(
            pltpu.make_async_copy(wq_hbm.at[pl.ds(a, b - a)], wq.at[pl.ds(a, b - a)], wq_sem.at[c])
        )
        loads[-1].start()
    load_out = pltpu.make_async_copy(wo_hbm, wo, wo_sem)
    load_out.start()

    load_lat.wait()
    for load in gains:
        load.wait()
    values = lat[...].astype(F32).reshape(tokens, model)
    center = values - jnp.mean(values, axis=-1, keepdims=True)
    spread = jnp.mean(center * center, axis=-1, keepdims=True)
    normed = center * lax.rsqrt(spread + 1e-06) * ln_ref[...].reshape(1, model)
    xs[...] = normed.reshape(n, per, model).astype(BF16)
    xr[pl.ds(me, 1)] = xs[pl.ds(me, 1)]

    pl.semaphore_wait(barrier, n - 1)

    def send_all(src, dst, send, recv, c, a, b):
        for to in peers:
            pltpu.make_async_remote_copy(
                src_ref=src.at[to, :, pl.ds(a, b - a)],
                dst_ref=dst.at[me, :, pl.ds(a, b - a)],
                send_sem=send.at[c],
                recv_sem=recv.at[c],
                device_id={"frame": to},
                device_id_type=MESH,
            ).start()

    def all_copies(src, dst, send, recv, c, a, b):
        return pltpu.make_async_remote_copy(
            src_ref=src.at[pl.ds(0, n - 1), :, pl.ds(a, b - a)],
            dst_ref=dst.at[pl.ds(0, n - 1), :, pl.ds(a, b - a)],
            send_sem=send.at[c],
            recv_sem=recv.at[c],
            device_id={"frame": peers[0]},
            device_id_type=MESH,
        )

    def wait_recv_all(src, dst, send, recv, c, a, b):
        all_copies(src, dst, send, recv, c, a, b).wait_recv()

    def wait_send_all(src, dst, send, recv, c, a, b):
        all_copies(src, dst, send, recv, c, a, b).wait_send()

    for c, (a, b) in enumerate(in_parts):
        send_all(xs, xr, s1, r1, c, a, b)

    entry = lax.broadcasted_iota(jnp.int32, (HEAD_DIM, model), 0)
    place = lax.broadcasted_iota(jnp.int32, (HEAD_DIM, model), 1)
    picked = entry == place
    for h in range(1, HEADS):
        picked = picked | (entry + h * HEAD_DIM == place)
    repeat = picked.astype(F32)

    def whole_gain(ref):
        rows8 = jnp.broadcast_to(ref[...].reshape(1, HEAD_DIM), (8, HEAD_DIM))
        return jnp.dot(
            rows8, repeat, preferred_element_type=F32, precision=lax.Precision.HIGHEST
        )[0:1]

    q_gain = whole_gain(qg_ref)
    k_gain = whole_gain(kg_ref)

    row_i = lax.broadcasted_iota(jnp.int32, (tokens, tokens), 0)
    col_i = lax.broadcasted_iota(jnp.int32, (tokens, tokens), 1)
    same = lax.rem(row_i, per) == lax.rem(col_i, per)

    def arrived(c, a, b):
        wait_recv_all(xs, xr, s1, r1, c, a, b)
        loads[c].wait()
        return xr[:, :, a:b].astype(F32).reshape(tokens, b - a).astype(BF16)

    width = 3 * model
    step = model // 3
    for c, (a, b) in enumerate(in_parts[:-1]):
        part = arrived(c, a, b)
        for col in range(0, width, step):
            product = jnp.dot(part, wq[a:b, col : col + step], preferred_element_type=F32)
            if c == 0:
                acc[:, col : col + step] = product
            else:
                acc[:, col : col + step] += product

    last, (a_in, b_in) = len(in_parts) - 1, in_parts[-1]
    part = arrived(last, a_in, b_in)

    def head_mask(h, lo, hi):
        at = lax.broadcasted_iota(jnp.int32, (tokens, hi - lo), 1) + lo
        return (at >= h * HEAD_DIM) & (at < (h + 1) * HEAD_DIM)

    probs = {}
    done = 0
    for c, (a, b) in enumerate(out_parts):
        piece = slice(MID_CUTS[c], MID_CUTS[c + 1])
        for third in range(3):
            cols = slice(third * model + piece.start, third * model + piece.stop)
            acc[:, cols] += jnp.dot(part, wq[a_in:b_in, cols], preferred_element_type=F32)

        first, done = done, piece.stop // HEAD_DIM
        count = done - first
        lo = first * HEAD_DIM // LANES * LANES
        hi = -(-done * HEAD_DIM // LANES) * LANES
        span = hi - lo
        lane = lax.broadcasted_iota(jnp.int32, (span, LANES), 0) + lo
        head = lax.broadcasted_iota(jnp.int32, (span, LANES), 1)
        start = (head + first) * HEAD_DIM
        gather = ((head < count) & (lane >= start) & (lane < start + HEAD_DIM)).astype(F32)
        gather = gather.astype(BF16)
        head = lax.rem(lax.broadcasted_iota(jnp.int32, (2 * LANES, span), 0), LANES)
        lane = lax.broadcasted_iota(jnp.int32, (2 * LANES, span), 1) + lo
        start = (head + first) * HEAD_DIM
        expand = ((head < count) & (lane >= start) & (lane < start + HEAD_DIM)).astype(F32)
        expand = expand.astype(BF16)

        def head_norm(base, gain):
            block = acc[:, base + lo : base + hi]
            square = block * block
            high = square.astype(BF16)
            low = (square - high.astype(F32)).astype(BF16)
            sums = jnp.dot(high, gather, preferred_element_type=F32)
            sums += jnp.dot(low, gather, preferred_element_type=F32)
            scale = lax.rsqrt(sums * (1.0 / HEAD_DIM) + 1e-06)
            high = scale.astype(BF16)
            low = (scale - high.astype(F32)).astype(BF16)
            scale = jnp.dot(
                jnp.concatenate([high, low], axis=1), expand, preferred_element_type=F32
            )
            return (block * scale * gain[:, lo:hi]).astype(BF16)

        qn[:, :span] = head_norm(0, q_gain)
        kn[:, :span] = head_norm(model, k_gain)

        for h in range(first, done):
            at = h * HEAD_DIM // LANES * LANES
            end = -(-(h + 1) * HEAD_DIM // LANES) * LANES
            mask = head_mask(h, at, end)
            query = jnp.where(mask, qn[:, at - lo : end - lo].astype(F32), 0.0).astype(BF16)
            scores = lax.dot_general(
                query,
                kn[:, at - lo : end - lo],
                (((1,), (1,)), ((), ())),
                preferred_element_type=F32,
            ) * (HEAD_DIM**-0.5)
            weights = jnp.where(same, jnp.exp(scores), 0.0)
            total = jnp.sum(weights, axis=-1, keepdims=True)
            probs[h] = (weights * (1.0 / total)).astype(BF16)

        for tile in range(a, b, LANES):
            out_tile = None
            for h in range(tile // HEAD_DIM, (tile + LANES - 1) // HEAD_DIM + 1):
                mask = head_mask(h, tile, tile + LANES)
                value = acc[:, 2 * model + tile : 2 * model + tile + LANES]
                value = jnp.where(mask, value, 0.0).astype(BF16)
                term = jnp.dot(probs[h], value, preferred_element_type=F32)
                out_tile = term if out_tile is None else out_tile + term
            ys[:, :, tile : tile + LANES] = out_tile.reshape(n, per, LANES).astype(BF16)
        send_all(ys, yr, s2, r2, c, a, b)
    yr[pl.ds(me, 1)] = ys[pl.ds(me, 1)]

    load_out.wait()
    for c, (a, b) in enumerate(in_parts):
        wait_send_all(xs, xr, s1, r1, c, a, b)
    for c, (a, b) in enumerate(out_parts):
        wait_recv_all(ys, yr, s2, r2, c, a, b)
        part = yr[:, :, a:b].astype(F32).reshape(tokens, b - a).astype(BF16)
        product = jnp.dot(part, wo[a:b, :], preferred_element_type=F32)
        if c == 0:
            acc[:, :model] = product
        elif c < len(out_parts) - 1:
            acc[:, :model] += product
        else:
            branch = lat[...].astype(F32).reshape(tokens, model)
            product = acc[:, :model] + product
            out_ref[...] = (branch + product).reshape(rows, columns, model).astype(BF16)
    for c, (a, b) in enumerate(out_parts):
        wait_send_all(ys, yr, s2, r2, c, a, b)


def fused(n, latent, ln_gain, q_gain, k_gain, w_qkv, w_out):
    rows, columns, model = latent.shape
    tokens = rows * columns
    per = tokens // n
    vmem = pl.BlockSpec(memory_space=pltpu.VMEM)
    hbm = pl.BlockSpec(memory_space=pltpu.HBM)
    block = pltpu.VMEM((n, per, model), BF16)
    ins, outs = len(IN_CUTS) - 1, len(OUT_CUTS) - 1
    return pl.pallas_call(
        functools.partial(kernel, n),
        out_shape=jax.ShapeDtypeStruct(latent.shape, BF16),
        in_specs=[hbm] * 6,
        out_specs=vmem,
        scratch_shapes=[
            pltpu.VMEM(latent.shape, BF16),
            pltpu.VMEM(ln_gain.shape, F32),
            pltpu.VMEM(q_gain.shape, F32),
            pltpu.VMEM(k_gain.shape, F32),
            block,
            block,
            block,
            block,
            pltpu.VMEM(w_qkv.shape, BF16),
            pltpu.VMEM(w_out.shape, BF16),
            pltpu.VMEM((tokens, w_qkv.shape[1]), F32),
            pltpu.VMEM((tokens, SPAN), BF16),
            pltpu.VMEM((tokens, SPAN), BF16),
            pltpu.SemaphoreType.DMA,
            pltpu.SemaphoreType.DMA((3,)),
            pltpu.SemaphoreType.DMA((ins,)),
            pltpu.SemaphoreType.DMA,
            pltpu.SemaphoreType.DMA((ins,)),
            pltpu.SemaphoreType.DMA((ins,)),
            pltpu.SemaphoreType.DMA((outs,)),
            pltpu.SemaphoreType.DMA((outs,)),
        ],
        compiler_params=pltpu.CompilerParams(
            collective_id=0, has_side_effects=True, vmem_limit_bytes=VMEM_BYTES
        ),
    )(
        *(
            pltpu.with_memory_space_constraint(value, pltpu.HBM)
            for value in (latent, ln_gain, q_gain, k_gain, w_qkv, w_out)
        )
    )


def layer_norm(rows, ln_gain):
    values = rows.astype(jnp.float32)
    center = values - jnp.mean(values, axis=-1, keepdims=True)
    spread = jnp.mean(center * center, axis=-1, keepdims=True)
    return (center * lax.rsqrt(spread + 1e-06) * ln_gain).astype(jnp.bfloat16)


def head_norm(values, gain):
    shaped = values.reshape(values.shape[:-1] + (HEADS, HEAD_DIM))
    mean_sq = jnp.mean(shaped * shaped, axis=-1, keepdims=True)
    return (shaped * lax.rsqrt(mean_sq + 1e-06) * gain).astype(jnp.bfloat16).reshape(values.shape)


def project(normed, w_qkv, q_gain, k_gain):
    width = normed.shape[-1]
    mixed = jnp.dot(normed.reshape(-1, width), w_qkv, preferred_element_type=jnp.float32)
    mixed = mixed.reshape(normed.shape[:-1] + (3 * width,))
    query = head_norm(mixed[..., :width], q_gain)
    keys = head_norm(mixed[..., width : 2 * width], k_gain)
    values = mixed[..., 2 * width :].astype(jnp.bfloat16)
    return (query, keys, values)


def attend(query, keys, values):
    lead = query.shape[0]
    others = query.shape[1]
    q_four = query.reshape(lead, others, HEADS, HEAD_DIM)
    k_four = keys.reshape(lead, others, HEADS, HEAD_DIM)
    v_four = values.reshape(lead, others, HEADS, HEAD_DIM)
    scores = jnp.einsum(
        "tshe,ushe->shtu", q_four, k_four, preferred_element_type=jnp.float32
    ) * HEAD_DIM ** (-0.5)
    weights = jnp.exp(scores)
    weights = (weights / jnp.sum(weights, axis=-1, keepdims=True)).astype(jnp.bfloat16)
    mixed = jnp.einsum("shtu,ushe->tshe", weights, v_four, preferred_element_type=jnp.float32)
    return mixed.astype(jnp.bfloat16).reshape(query.shape)


def body(latent, ln_gain, q_gain, k_gain, w_qkv, w_out):
    device_count = lax.axis_size("frame")
    rows, columns, model = latent.shape
    positions = rows * columns
    per_peer = positions // device_count
    if per_peer % 8 == 0:
        return fused(device_count, latent, ln_gain, q_gain, k_gain, w_qkv, w_out)
    flat = latent.reshape(positions, model)
    normed = layer_norm(flat, ln_gain)
    query, keys, values = project(
        lax.all_to_all(
            normed.reshape(device_count, per_peer, model),
            "frame",
            split_axis=0,
            concat_axis=0,
            tiled=True,
        ),
        w_qkv,
        q_gain,
        k_gain,
    )
    mixed = attend(query, keys, values)
    returned = lax.all_to_all(mixed, "frame", split_axis=0, concat_axis=0, tiled=True)
    attended = returned.reshape(positions, model)
    branch = jnp.dot(attended, w_out, preferred_element_type=jnp.float32)
    result = flat.astype(jnp.float32) + branch
    return result.astype(jnp.bfloat16).reshape(latent.shape)


def solution(mesh):
    placed = (P(("groups", "frame"), None, None), P(), P(), P(), P(), P())
    return jax.shard_map(
        body,
        mesh=mesh,
        in_specs=placed,
        out_specs=P(("groups", "frame"), None, None),
        check_vma=False,
    )
```

```python
import functools

import jax
import jax.numpy as jnp
from jax import lax
from jax.experimental import pallas as pl
from jax.experimental.pallas import tpu as pltpu
from jax.sharding import PartitionSpec as P

HEADS = 16
HEAD_DIM = 72
LANES = 128
IN_CUTS = (0, 1152)
MID_CUTS = (0, 384, 768, 1152)
OUT_CUTS = (0, 256, 640, 1152)
SPAN = 512
VMEM_BYTES = 30000000
MESH = pl.DeviceIdType.MESH
F32 = jnp.float32
BF16 = jnp.bfloat16


def kernel(
    n,
    lat_hbm,
    ln_hbm,
    qg_hbm,
    kg_hbm,
    wq_hbm,
    wo_hbm,
    out_ref,
    lat,
    ln_ref,
    qg_ref,
    kg_ref,
    xs,
    xr,
    ys,
    yr,
    wq,
    wo,
    acc,
    qn,
    kn,
    lat_sem,
    gain_sem,
    wq_sem,
    wo_sem,
    s1,
    r1,
    s2,
    r2,
):
    rows, columns, model = lat_hbm.shape
    tokens = rows * columns
    per = tokens // n
    me = lax.axis_index("frame")
    in_parts = list(zip(IN_CUTS[:-1], IN_CUTS[1:]))
    out_parts = list(zip(OUT_CUTS[:-1], OUT_CUTS[1:]))

    barrier = pltpu.get_barrier_semaphore()

    steps = range(1, n)
    peers = [lax.rem(me + k, n) for k in steps]
    for to in peers:
        pl.semaphore_signal(barrier, inc=1, device_id={"frame": to}, device_id_type=MESH)

    load_lat = pltpu.make_async_copy(lat_hbm, lat, lat_sem)
    load_lat.start()
    gains = [
        pltpu.make_async_copy(src, dst, gain_sem.at[i])
        for i, (src, dst) in enumerate(((ln_hbm, ln_ref), (qg_hbm, qg_ref), (kg_hbm, kg_ref)))
    ]
    for load in gains:
        load.start()
    loads = []
    for c, (a, b) in enumerate(in_parts):
        loads.append(
            pltpu.make_async_copy(wq_hbm.at[pl.ds(a, b - a)], wq.at[pl.ds(a, b - a)], wq_sem.at[c])
        )
        loads[-1].start()
    load_out = pltpu.make_async_copy(wo_hbm, wo, wo_sem)
    load_out.start()

    load_lat.wait()
    for load in gains:
        load.wait()
    values = lat[...].astype(F32).reshape(tokens, model)
    center = values - jnp.mean(values, axis=-1, keepdims=True)
    spread = jnp.mean(center * center, axis=-1, keepdims=True)
    normed = center * lax.rsqrt(spread + 1e-06) * ln_ref[...].reshape(1, model)
    xs[...] = normed.reshape(n, per, model).astype(BF16)
    xr[pl.ds(me, 1)] = xs[pl.ds(me, 1)]

    pl.semaphore_wait(barrier, n - 1)

    def send_all(src, dst, send, recv, c, a, b):
        for to in peers:
            pltpu.make_async_remote_copy(
                src_ref=src.at[to, :, pl.ds(a, b - a)],
                dst_ref=dst.at[me, :, pl.ds(a, b - a)],
                send_sem=send.at[c],
                recv_sem=recv.at[c],
                device_id={"frame": to},
                device_id_type=MESH,
            ).start()

    def all_copies(src, dst, send, recv, c, a, b):
        return pltpu.make_async_remote_copy(
            src_ref=src.at[pl.ds(0, n - 1), :, pl.ds(a, b - a)],
            dst_ref=dst.at[pl.ds(0, n - 1), :, pl.ds(a, b - a)],
            send_sem=send.at[c],
            recv_sem=recv.at[c],
            device_id={"frame": peers[0]},
            device_id_type=MESH,
        )

    def wait_recv_all(src, dst, send, recv, c, a, b):
        all_copies(src, dst, send, recv, c, a, b).wait_recv()

    def wait_send_all(src, dst, send, recv, c, a, b):
        all_copies(src, dst, send, recv, c, a, b).wait_send()

    for c, (a, b) in enumerate(in_parts):
        send_all(xs, xr, s1, r1, c, a, b)

    entry = lax.broadcasted_iota(jnp.int32, (HEAD_DIM, model), 0)
    place = lax.broadcasted_iota(jnp.int32, (HEAD_DIM, model), 1)
    picked = entry == place
    for h in range(1, HEADS):
        picked = picked | (entry + h * HEAD_DIM == place)
    repeat = picked.astype(F32)

    def whole_gain(ref):
        rows8 = jnp.broadcast_to(ref[...].reshape(1, HEAD_DIM), (8, HEAD_DIM))
        return jnp.dot(
            rows8, repeat, preferred_element_type=F32, precision=lax.Precision.HIGHEST
        )[0:1]

    q_gain = whole_gain(qg_ref)
    k_gain = whole_gain(kg_ref)

    row_i = lax.broadcasted_iota(jnp.int32, (tokens, tokens), 0)
    col_i = lax.broadcasted_iota(jnp.int32, (tokens, tokens), 1)
    same = lax.rem(row_i, per) == lax.rem(col_i, per)

    def arrived(c, a, b):
        wait_recv_all(xs, xr, s1, r1, c, a, b)
        loads[c].wait()
        return xr[:, :, a:b].astype(F32).reshape(tokens, b - a).astype(BF16)

    width = 3 * model
    step = model // 3
    for c, (a, b) in enumerate(in_parts[:-1]):
        part = arrived(c, a, b)
        for col in range(0, width, step):
            product = jnp.dot(part, wq[a:b, col : col + step], preferred_element_type=F32)
            if c == 0:
                acc[:, col : col + step] = product
            else:
                acc[:, col : col + step] += product

    last, (a_in, b_in) = len(in_parts) - 1, in_parts[-1]
    part = arrived(last, a_in, b_in)

    def head_mask(h, lo, hi):
        at = lax.broadcasted_iota(jnp.int32, (tokens, hi - lo), 1) + lo
        return (at >= h * HEAD_DIM) & (at < (h + 1) * HEAD_DIM)

    probs = {}
    done = 0
    for c, (a, b) in enumerate(out_parts):
        piece = slice(MID_CUTS[c], MID_CUTS[c + 1])
        for third in range(3):
            cols = slice(third * model + piece.start, third * model + piece.stop)
            product = jnp.dot(part, wq[a_in:b_in, cols], preferred_element_type=F32)
            acc[:, cols] = product if last == 0 else acc[:, cols] + product

        first, done = done, piece.stop // HEAD_DIM
        count = done - first
        lo = first * HEAD_DIM // LANES * LANES
        hi = -(-done * HEAD_DIM // LANES) * LANES
        span = hi - lo
        lane = lax.broadcasted_iota(jnp.int32, (span, LANES), 0) + lo
        head = lax.broadcasted_iota(jnp.int32, (span, LANES), 1)
        start = (head + first) * HEAD_DIM
        gather = ((head < count) & (lane >= start) & (lane < start + HEAD_DIM)).astype(F32)
        gather = gather.astype(BF16)
        head = lax.rem(lax.broadcasted_iota(jnp.int32, (2 * LANES, span), 0), LANES)
        lane = lax.broadcasted_iota(jnp.int32, (2 * LANES, span), 1) + lo
        start = (head + first) * HEAD_DIM
        expand = ((head < count) & (lane >= start) & (lane < start + HEAD_DIM)).astype(F32)
        expand = expand.astype(BF16)

        def head_norm(base, gain):
            block = acc[:, base + lo : base + hi]
            square = block * block
            high = square.astype(BF16)
            low = (square - high.astype(F32)).astype(BF16)
            sums = jnp.dot(high, gather, preferred_element_type=F32)
            sums += jnp.dot(low, gather, preferred_element_type=F32)
            scale = lax.rsqrt(sums * (1.0 / HEAD_DIM) + 1e-06)
            high = scale.astype(BF16)
            low = (scale - high.astype(F32)).astype(BF16)
            scale = jnp.dot(
                jnp.concatenate([high, low], axis=1), expand, preferred_element_type=F32
            )
            return (block * scale * gain[:, lo:hi]).astype(BF16)

        qn[:, :span] = head_norm(0, q_gain)
        kn[:, :span] = head_norm(model, k_gain)

        for h in range(first, done):
            at = h * HEAD_DIM // LANES * LANES
            end = -(-(h + 1) * HEAD_DIM // LANES) * LANES
            mask = head_mask(h, at, end)
            query = jnp.where(mask, qn[:, at - lo : end - lo].astype(F32), 0.0).astype(BF16)
            scores = lax.dot_general(
                query,
                kn[:, at - lo : end - lo],
                (((1,), (1,)), ((), ())),
                preferred_element_type=F32,
            ) * (HEAD_DIM**-0.5)
            weights = jnp.where(same, jnp.exp(scores), 0.0)
            total = jnp.sum(weights, axis=-1, keepdims=True)
            probs[h] = (weights * (1.0 / total)).astype(BF16)

        for tile in range(a, b, LANES):
            out_tile = None
            for h in range(tile // HEAD_DIM, (tile + LANES - 1) // HEAD_DIM + 1):
                mask = head_mask(h, tile, tile + LANES)
                value = acc[:, 2 * model + tile : 2 * model + tile + LANES]
                value = jnp.where(mask, value, 0.0).astype(BF16)
                term = jnp.dot(probs[h], value, preferred_element_type=F32)
                out_tile = term if out_tile is None else out_tile + term
            ys[:, :, tile : tile + LANES] = out_tile.reshape(n, per, LANES).astype(BF16)
        send_all(ys, yr, s2, r2, c, a, b)
    yr[pl.ds(me, 1)] = ys[pl.ds(me, 1)]

    load_out.wait()
    for c, (a, b) in enumerate(in_parts):
        wait_send_all(xs, xr, s1, r1, c, a, b)
    for c, (a, b) in enumerate(out_parts):
        wait_recv_all(ys, yr, s2, r2, c, a, b)
        part = yr[:, :, a:b].astype(F32).reshape(tokens, b - a).astype(BF16)
        product = jnp.dot(part, wo[a:b, :], preferred_element_type=F32)
        if c == 0:
            acc[:, :model] = product
        elif c < len(out_parts) - 1:
            acc[:, :model] += product
        else:
            branch = lat[...].astype(F32).reshape(tokens, model)
            product = acc[:, :model] + product
            out_ref[...] = (branch + product).reshape(rows, columns, model).astype(BF16)
    for c, (a, b) in enumerate(out_parts):
        wait_send_all(ys, yr, s2, r2, c, a, b)


def fused(n, latent, ln_gain, q_gain, k_gain, w_qkv, w_out):
    rows, columns, model = latent.shape
    tokens = rows * columns
    per = tokens // n
    vmem = pl.BlockSpec(memory_space=pltpu.VMEM)
    hbm = pl.BlockSpec(memory_space=pltpu.HBM)
    block = pltpu.VMEM((n, per, model), BF16)
    ins, outs = len(IN_CUTS) - 1, len(OUT_CUTS) - 1
    return pl.pallas_call(
        functools.partial(kernel, n),
        out_shape=jax.ShapeDtypeStruct(latent.shape, BF16),
        in_specs=[hbm] * 6,
        out_specs=vmem,
        scratch_shapes=[
            pltpu.VMEM(latent.shape, BF16),
            pltpu.VMEM(ln_gain.shape, F32),
            pltpu.VMEM(q_gain.shape, F32),
            pltpu.VMEM(k_gain.shape, F32),
            block,
            block,
            block,
            block,
            pltpu.VMEM(w_qkv.shape, BF16),
            pltpu.VMEM(w_out.shape, BF16),
            pltpu.VMEM((tokens, w_qkv.shape[1]), F32),
            pltpu.VMEM((tokens, SPAN), BF16),
            pltpu.VMEM((tokens, SPAN), BF16),
            pltpu.SemaphoreType.DMA,
            pltpu.SemaphoreType.DMA((3,)),
            pltpu.SemaphoreType.DMA((ins,)),
            pltpu.SemaphoreType.DMA,
            pltpu.SemaphoreType.DMA((ins,)),
            pltpu.SemaphoreType.DMA((ins,)),
            pltpu.SemaphoreType.DMA((outs,)),
            pltpu.SemaphoreType.DMA((outs,)),
        ],
        compiler_params=pltpu.CompilerParams(
            collective_id=0, has_side_effects=True, vmem_limit_bytes=VMEM_BYTES
        ),
    )(
        *(
            pltpu.with_memory_space_constraint(value, pltpu.HBM)
            for value in (latent, ln_gain, q_gain, k_gain, w_qkv, w_out)
        )
    )


def layer_norm(rows, ln_gain):
    values = rows.astype(jnp.float32)
    center = values - jnp.mean(values, axis=-1, keepdims=True)
    spread = jnp.mean(center * center, axis=-1, keepdims=True)
    return (center * lax.rsqrt(spread + 1e-06) * ln_gain).astype(jnp.bfloat16)


def head_norm(values, gain):
    shaped = values.reshape(values.shape[:-1] + (HEADS, HEAD_DIM))
    mean_sq = jnp.mean(shaped * shaped, axis=-1, keepdims=True)
    return (shaped * lax.rsqrt(mean_sq + 1e-06) * gain).astype(jnp.bfloat16).reshape(values.shape)


def project(normed, w_qkv, q_gain, k_gain):
    width = normed.shape[-1]
    mixed = jnp.dot(normed.reshape(-1, width), w_qkv, preferred_element_type=jnp.float32)
    mixed = mixed.reshape(normed.shape[:-1] + (3 * width,))
    query = head_norm(mixed[..., :width], q_gain)
    keys = head_norm(mixed[..., width : 2 * width], k_gain)
    values = mixed[..., 2 * width :].astype(jnp.bfloat16)
    return (query, keys, values)


def attend(query, keys, values):
    lead = query.shape[0]
    others = query.shape[1]
    q_four = query.reshape(lead, others, HEADS, HEAD_DIM)
    k_four = keys.reshape(lead, others, HEADS, HEAD_DIM)
    v_four = values.reshape(lead, others, HEADS, HEAD_DIM)
    scores = jnp.einsum(
        "tshe,ushe->shtu", q_four, k_four, preferred_element_type=jnp.float32
    ) * HEAD_DIM ** (-0.5)
    weights = jnp.exp(scores)
    weights = (weights / jnp.sum(weights, axis=-1, keepdims=True)).astype(jnp.bfloat16)
    mixed = jnp.einsum("shtu,ushe->tshe", weights, v_four, preferred_element_type=jnp.float32)
    return mixed.astype(jnp.bfloat16).reshape(query.shape)


def body(latent, ln_gain, q_gain, k_gain, w_qkv, w_out):
    device_count = lax.axis_size("frame")
    rows, columns, model = latent.shape
    positions = rows * columns
    per_peer = positions // device_count
    if per_peer % 8 == 0:
        return fused(device_count, latent, ln_gain, q_gain, k_gain, w_qkv, w_out)
    flat = latent.reshape(positions, model)
    normed = layer_norm(flat, ln_gain)
    query, keys, values = project(
        lax.all_to_all(
            normed.reshape(device_count, per_peer, model),
            "frame",
            split_axis=0,
            concat_axis=0,
            tiled=True,
        ),
        w_qkv,
        q_gain,
        k_gain,
    )
    mixed = attend(query, keys, values)
    returned = lax.all_to_all(mixed, "frame", split_axis=0, concat_axis=0, tiled=True)
    attended = returned.reshape(positions, model)
    branch = jnp.dot(attended, w_out, preferred_element_type=jnp.float32)
    result = flat.astype(jnp.float32) + branch
    return result.astype(jnp.bfloat16).reshape(latent.shape)


def solution(mesh):
    placed = (P(("groups", "frame"), None, None), P(), P(), P(), P(), P())
    return jax.shard_map(
        body,
        mesh=mesh,
        in_specs=placed,
        out_specs=P(("groups", "frame"), None, None),
        check_vma=False,
    )
```
